512 devices in a mesh: dp: 8 (over z_hi, core), ctx: 64 (over z_lo, y, x).
Axes of the slice: x: 4, y: 4, z: 16 (z_hi: 4, z_lo: 4; z = z_hi * 4 + z_lo), core: 2. Of those that a mesh axis runs over, the one named last changes fastest.
Arguments:
- pre_gate: bfloat16 [8, 8192, 2048], P('dp', 'ctx'), may hold values from -6 to 6
- post_gate: bfloat16 [8, 8192, 2048], P('dp', 'ctx'), may hold values from -6 to 6
- values: bfloat16 [8, 8192, 2048], P('dp', 'ctx'), may hold values from -6 to 6
- conv_out: bfloat16 [8, 8192, 2048], P('dp', 'ctx'), may hold values from -6 to 6
- grad_out: bfloat16 [8, 8192, 2048], P('dp', 'ctx'), may hold values from -6 to 6
- filter_param: bfloat16 [2048, 8192], P('ctx'), may hold values from -6 to 6
Outputs:
- d_pre_gate: bfloat16 [8, 8192, 2048], P('dp', 'ctx')
- d_post_gate: bfloat16 [8, 8192, 2048], P('dp', 'ctx')
- d_values: bfloat16 [8, 8192, 2048], P('dp', 'ctx')
- d_filter: float32 [2048, 8192], P(('ctx', 'dp'))
The draws below stay inside these ranges and needn't reach their ends.
All inputs are finite; a program needn't handle non-finite values.
Results may differ from the reference program's by a relative error of at most 0.0058.
Values may be sent and summed in bfloat16 or wider, within the bound.
No kernel may reach another device: no remote copies, remote signals or barrier semaphores. Data moves between devices by JAX's collectives and lax.ppermute only.
A program may use at most 64 MiB of HBM per device.

```python
import math
import jax
import jax.numpy as jnp
from jax import lax

C = 2048
SEQ = 8192
BATCH = 8


def level_of(rng, dims, split, least, top_value):
    def one(dim, blocks):
        draws = jax.random.uniform(jax.random.fold_in(jax.random.fold_in(rng, 6), dim), (blocks,), jnp.float32, least / len(split), top_value / len(split))
        return jnp.repeat(jnp.exp(draws), dims[dim] // blocks).reshape((-1,) + (1,) * (len(dims) - dim - 1))

    loudness = one(*split[0])
    for cut in split[1:]:
        loudness = loudness * one(*cut)
    return loudness


def bell_draw(stream_key, shape, spread, most, pieces=(), kind=jnp.bfloat16):
    gain = level_of(stream_key, shape, pieces, -0.22, 0.18) if pieces else 1.0
    values = jax.random.normal(stream_key, shape, jnp.float32) * spread * gain
    return jnp.minimum(jnp.maximum(values, -most), most).astype(kind)


def setup_inputs(seed: int = 0) -> dict:
    key_list = jax.random.split(jax.random.key(seed), 7)
    return {
        "pre_gate": bell_draw(key_list[0], (BATCH, SEQ, C), 1.0, 6.0, ((0, 8), (1, 64))),
        "post_gate": bell_draw(key_list[1], (BATCH, SEQ, C), 1.0, 6.0, ((0, 8), (1, 64))),
        "values": bell_draw(key_list[2], (BATCH, SEQ, C), 1.0, 6.0, ((0, 8), (1, 64))),
        "conv_out": bell_draw(key_list[3], (BATCH, SEQ, C), 1.0, 6.0, ((0, 8), (1, 64))),
        "grad_out": bell_draw(key_list[4], (BATCH, SEQ, C), 1.0, 6.0, ((0, 8), (1, 64))),
        "filter_param": bell_draw(key_list[5], (C, SEQ), 1.0, 6.0, ((0, 64),)),
    }


def reference(pre_gate, post_gate, values, conv_out, grad_out, filter_param):
    whole = 2 * SEQ
    kernel = filter_param.astype(jnp.float32) * SEQ ** (-0.5)
    kernel_spec = jnp.fft.fft(kernel, n=whole, axis=1)

    def one_sequence(total, items):
        gate_row, post_row, value_row, out_row, grad_row = items
        mixed = (gate_row.astype(jnp.float32) * value_row.astype(jnp.float32)).astype(jnp.bfloat16)
        grad_conv = (grad_row.astype(jnp.float32) * post_row.astype(jnp.float32)).astype(jnp.bfloat16)
        mixed_spec = jnp.fft.fft(mixed.astype(jnp.float32).T, n=whole, axis=1)
        grad_spec = jnp.fft.fft(grad_conv.astype(jnp.float32).T, n=whole, axis=1)
        back = jnp.fft.ifft(jnp.conj(kernel_spec) * grad_spec, axis=1).real[:, :SEQ]
        back = back.T.astype(jnp.bfloat16).astype(jnp.float32)
        d_pre = (back * value_row.astype(jnp.float32)).astype(jnp.bfloat16)
        d_val = (back * gate_row.astype(jnp.float32)).astype(jnp.bfloat16)
        d_post = (grad_row.astype(jnp.float32) * out_row.astype(jnp.float32)).astype(jnp.bfloat16)
        term = jnp.fft.ifft(grad_spec * jnp.conj(mixed_spec), axis=1).real[:, :SEQ]
        return (total + term.astype(total.dtype), (d_pre, d_post, d_val))
    start = jnp.zeros((C, SEQ), jnp.float32)
    total, outs = lax.scan(one_sequence, start, (pre_gate, post_gate, values, conv_out, grad_out))
    d_filter = total * (1.0 / (BATCH * math.sqrt(SEQ)))
    return (outs[0], outs[1], outs[2], d_filter)
```

```python
import functools

import jax
import jax.numpy as jnp
from jax import lax
from jax.experimental import pallas as pl
from jax.experimental.pallas import tpu as pltpu
from jax.sharding import Mesh
from jax.sharding import PartitionSpec as P


L = 128
R = 64
CH = 32
DP = ("zh", "core")
CTX = ("zl", "y", "x")
F32 = jnp.float32
BF16 = jnp.bfloat16
VMEM_LIMIT = 10 << 20
GROUPS = ((0, 1), (2, 3))


def pre_body(x_ref, y_ref, send_ref):
    width = x_ref.shape[1]
    product = (x_ref[...].astype(F32) * y_ref[...].astype(F32)).astype(BF16)
    send_ref[...] = product.T.reshape(width // CH, CH, L)


def pre(x, y):
    channels = x.shape[1]
    width = 512
    block = pl.BlockSpec((L, width), lambda i: (0, i))
    return pl.pallas_call(
        pre_body,
        grid=(channels // width,),
        in_specs=[block] * 2,
        out_specs=pl.BlockSpec((width // CH, CH, L), lambda i: (i, 0, 0)),
        out_shape=jax.ShapeDtypeStruct((channels // CH, CH, L), BF16),
        cost_estimate=pl.CostEstimate(flops=0, bytes_accessed=3 * channels * L * 2, transcendentals=0),
    )(x, y)


def post_body(back_ref, gate_ref, value_ref, d_pre_ref, d_val_ref):
    width = gate_ref.shape[1]
    back = back_ref[...].reshape(width, L).T.astype(F32)
    d_pre_ref[...] = (back * value_ref[...].astype(F32)).astype(BF16)
    d_val_ref[...] = (back * gate_ref[...].astype(F32)).astype(BF16)


def post(back, gate, value):
    channels = gate.shape[1]
    width = 512
    block = pl.BlockSpec((L, width), lambda i: (0, i))
    shape = jax.ShapeDtypeStruct((L, channels), BF16)
    return pl.pallas_call(
        post_body,
        grid=(channels // width,),
        in_specs=[pl.BlockSpec((width // CH, CH, L), lambda i: (i, 0, 0)), block, block],
        out_specs=(block, block),
        out_shape=(shape, shape),
        cost_estimate=pl.CostEstimate(flops=0, bytes_accessed=5 * channels * L * 2, transcendentals=0),
        compiler_params=pltpu.CompilerParams(vmem_limit_bytes=VMEM_LIMIT),
        name="post",
    )(back, gate, value)


def widen(recv_ref, wide):
    def rows(r, _):
        at = pl.multiple_of(r * 8, 8)
        for c in range(0, CH, 16):
            x = recv_ref[pl.ds(at, 8), c : c + 16, :].astype(F32)
            wide[c : c + 16, pl.ds(at, 8), :] = jnp.swapaxes(x, 0, 1)
        return 0

    lax.fori_loop(0, R // 8, rows, 0)


def narrow(wide, send_ref):
    def rows(r, _):
        at = pl.multiple_of(r * 8, 8)
        for c in range(0, CH, 16):
            x = jnp.swapaxes(wide[c : c + 16, pl.ds(at, 8), :], 0, 1)
            send_ref[pl.ds(at, 8), c : c + 16, :] = x.astype(BF16)
        return 0

    lax.fori_loop(0, R // 8, rows, 0)


def correlate(count, load_grad, load_other, store, halves):
    lane8 = lax.broadcasted_iota(jnp.int32, (8, L), 1)
    sub8 = lax.broadcasted_iota(jnp.int32, (8, L), 0)
    lane16 = lax.broadcasted_iota(jnp.int32, (16, L), 1)
    row16 = lax.broadcasted_iota(jnp.int32, (16, L), 0)
    lane = lax.broadcasted_iota(jnp.int32, (R, L), 1)
    for gp, vp, w, rhs, acc in halves:
        gp[pl.ds(R, 8), :] = jnp.zeros((8, L), F32)
        vp[pl.ds(0, 8), :] = jnp.zeros((8, L), F32)
        w[pl.ds(4, 1)] = jnp.zeros((1, 128, L), BF16)

    def build(c, half):
        gp, vp, w, rhs, _ = halves[half]
        gp[pl.ds(0, R), :] = load_grad(c)
        vp[pl.ds(8, R), :] = load_other(c)
        rows = gp[pl.ds(0, R), :]
        following = gp[pl.ds(1, R), :]
        for u in range(8):
            x = rows
            if u:
                x = pltpu.roll(jnp.where(lane >= 16 * u, rows, following), L - 16 * u, 1)
            x = x.astype(BF16)
            for t in range(4):
                w[t, pl.ds(16 * u, 16), :] = x[16 * t : 16 * t + 16]
        for j in range(R):
            h, i = divmod(j, 16)
            here = vp[pl.ds(8 + j, 8, stride=0), :]
            before = vp[pl.ds(7 + j, 8, stride=0), :]
            shifted = [
                pltpu.roll(jnp.where(lane8 < L - 8 * p - sub8, here, before), 8 * p, 1, stride=1, stride_axis=0)
                for p in range(2)
            ]
            rhs[h, pl.ds(16 * i, 16), :] = jnp.concatenate(shifted, axis=0).astype(BF16)

    def multiply(half):
        _, _, w, rhs, acc = halves[half]
        for group in GROUPS:
            depth = 4 - group[0]
            lhs = jnp.concatenate(
                [jnp.concatenate([w[min(p + h, 4)] for h in range(depth)], axis=1) for p in group], axis=0
            )
            cols = jnp.concatenate([rhs[h] for h in range(depth)], axis=1)
            out = lax.dot_general(lhs, cols, (((1,), (1,)), ((), ())), preferred_element_type=F32)
            for n, p in enumerate(group):
                acc[0, p] = out[128 * n : 128 * n + 128, :L]
                acc[1, p] = out[128 * n : 128 * n + 128, L:]

    def finish(c, half):
        _, _, _, _, acc = halves[half]
        tops = []
        for u in range(8):
            lo, hi = ([acc[k, p, pl.ds(16 * u, 16), :] for p in range(4)] for k in range(2))
            lo[0] = jnp.where(row16 >= lane16 // 16, lo[0], 0.0)
            hi[0] = jnp.where(row16 >= lane16 // 16 + 8, hi[0], 0.0)
            hi = jnp.concatenate(hi, axis=0)
            tops.append(jnp.concatenate(lo, axis=0) + jnp.concatenate([hi[8:], hi[:8]], axis=0))

        def pair(p, q, width):
            low = (lane & width) == 0
            a = jnp.where(low, p, q)
            b = jnp.where(low, q, p)
            right = pltpu.roll(b, width, 1)
            left = right if 2 * width == L else pltpu.roll(b, L - width, 1)
            return jnp.where(low, a, right) + pltpu.roll(jnp.where(low, left, a), R - width // 16, 0)

        fours = [pair(tops[u], tops[u + 4], 64) for u in range(4)]
        twos = [pair(fours[u], fours[u + 2], 32) for u in range(2)]
        store(c, pair(twos[0], twos[1], 16))

    build(0, 0)

    def step(n, _):
        c = 2 * n
        multiply(0)
        build(c + 1, 1)
        finish(jnp.maximum(c - 1, 0), 1)
        multiply(1)
        build(jnp.minimum(c + 2, count - 1), 0)
        finish(c, 0)
        return 0

    lax.fori_loop(0, count // 2, step, 0)
    finish(count - 1, 1)


HALF = [
    pltpu.VMEM((R + 8, L), F32),
    pltpu.VMEM((R + 8, L), F32),
    pltpu.VMEM((5, 128, L), BF16),
    pltpu.VMEM((4, 256, L), BF16),
    pltpu.VMEM((2, 4, 128, L), F32),
]
WHOLE = pl.BlockSpec(memory_space=pltpu.VMEM)
CONV_COST = pl.CostEstimate(flops=CH * 512 * 512 * 256 * 2, bytes_accessed=2 << 20, transcendentals=0)


def back_body(recv_ref, taps_ref, send_ref, grad_ref, wide, flat, *bufs, scale):
    widen(recv_ref, wide)

    def load_grad(c):
        rows = wide[c]
        grad_ref[c] = rows.astype(BF16)
        return rows

    def store(c, rows):
        flat[c] = rows * scale

    correlate(CH, load_grad, lambda c: taps_ref[c].astype(F32), store, (bufs[:5], bufs[5:]))
    narrow(flat, send_ref)


def conv_back(recv, taps, scale):
    return pl.pallas_call(
        functools.partial(back_body, scale=scale),
        in_specs=[WHOLE] * 2,
        out_specs=(WHOLE, WHOLE),
        out_shape=(jax.ShapeDtypeStruct((R, CH, L), BF16), jax.ShapeDtypeStruct((CH, R, L), BF16)),
        scratch_shapes=[pltpu.VMEM((CH, R, L), F32)] * 2 + HALF * 2,
        cost_estimate=CONV_COST,
        compiler_params=pltpu.CompilerParams(vmem_limit_bytes=VMEM_LIMIT),
        name="conv_back",
    )(recv, taps)


def channel_of(n, core):
    return lax.div(n, 4) * 8 + core * 4 + lax.rem(n, 4)


def term_first_body(core_ref, recv_ref, grad_ref, term_ref, mixed_ref, wide, *bufs, scale):
    widen(recv_ref, wide)

    def narrow_rows(c, _):
        mixed_ref[c] = wide[c].astype(BF16)
        return 0

    lax.fori_loop(0, CH, narrow_rows, 0)
    core = core_ref[0]

    def store(n, rows):
        term_ref[n] = rows * scale

    correlate(
        CH // 2,
        lambda n: grad_ref[channel_of(n, core)].astype(F32),
        lambda n: wide[channel_of(n, core)],
        store,
        (bufs[:5], bufs[5:]),
    )


def term_second_body(core_ref, mixed_ref, grad_ref, term_ref, *bufs, scale):
    core = core_ref[0]

    def store(n, rows):
        term_ref[n] = rows * scale

    correlate(
        CH // 2,
        lambda n: grad_ref[channel_of(n, core)].astype(F32),
        lambda n: mixed_ref[channel_of(n, core)].astype(F32),
        store,
        (bufs[:5], bufs[5:]),
    )


def conv_term(body, core, mixed, grad, scale, wide):
    rows = jax.ShapeDtypeStruct((CH, R, L), BF16)
    terms = jax.ShapeDtypeStruct((CH // 2, R, L), F32)
    return pl.pallas_call(
        functools.partial(body, scale=scale),
        in_specs=[pl.BlockSpec(memory_space=pltpu.SMEM)] + [WHOLE] * 2,
        out_specs=(WHOLE, WHOLE) if wide else WHOLE,
        out_shape=(terms, rows) if wide else terms,
        scratch_shapes=([pltpu.VMEM((CH, R, L), F32)] if wide else []) + HALF * 2,
        cost_estimate=CONV_COST,
        compiler_params=pltpu.CompilerParams(vmem_limit_bytes=VMEM_LIMIT),
    )(core, mixed, grad)


def sum_over_zh(both):
    zh = lax.axis_index("zh")
    count = lax.axis_size("zh")
    pick = functools.partial(lax.dynamic_index_in_dim, axis=0, keepdims=False)
    parts = []
    for shift in (2, 1, 3):
        ahead = [(i, (i + shift) % count) for i in range(count)]
        parts.append(lax.ppermute(pick(both, (zh + shift) % count).astype(BF16), "zh", ahead))
    return pick(both, zh) + (parts[0].astype(F32) + (parts[1].astype(F32) + parts[2].astype(F32)))


def local(pre_gate, post_gate, values, conv_out, grad_out, filter_param):
    gate, value, grad = pre_gate[0], values[0], grad_out[0]
    length = filter_param.shape[1]
    exchange = functools.partial(lax.all_to_all, axis_name=CTX, split_axis=0, concat_axis=0, tiled=True)
    grad_send = pre(grad, post_gate[0])
    grad_chan = exchange(grad_send)
    mixed_send = pre(gate, value)
    d_post = (grad.astype(F32) * conv_out[0].astype(F32)).astype(BF16)
    taps = filter_param.reshape(CH, R, L)
    mixed_chan = exchange(mixed_send)
    scale = length ** (-0.5)
    batch = lax.axis_size("zh") * lax.axis_size("core")
    back, grad_rows = conv_back(grad_chan, taps, scale)
    back = exchange(back)
    core = lax.axis_index("core").astype(jnp.int32)
    scale = scale / batch
    terms, mixed_rows = conv_term(term_first_body, (1 - core).reshape(1), mixed_chan, grad_rows, scale, True)
    terms = lax.ppermute(terms, "core", [(0, 1), (1, 0)])
    own = conv_term(term_second_body, core.reshape(1), mixed_rows, grad_rows, scale, False)
    d_filter = sum_over_zh((own + terms).reshape(4, 4, R, L)).reshape(4, length)
    d_pre, d_val = post(back, gate, value)
    return (d_pre[None], d_post[None], d_val[None], d_filter)


def solution(mesh):
    fine = Mesh(mesh.devices.reshape(4, 2, 4, 4, 4), DP + CTX)
    tokens = P(DP, CTX, None)
    return jax.shard_map(
        local,
        mesh=fine,
        in_specs=(tokens,) * 5 + (P(CTX, None),),
        out_specs=(tokens, tokens, tokens, P(CTX + DP, None)),
        check_vma=False,
    )
```

```python
import functools

import jax
import jax.numpy as jnp
from jax import lax
from jax.experimental import pallas as pl
from jax.experimental.pallas import tpu as pltpu
from jax.sharding import Mesh
from jax.sharding import PartitionSpec as P


L = 128
R = 64
CH = 32
DP = ("zh", "core")
CTX = ("zl", "y", "x")
F32 = jnp.float32
BF16 = jnp.bfloat16
VMEM_LIMIT = 16 << 20
GROUPS = ((0, 1), (2, 3))


def pre_body(gate_ref, value_ref, grad_ref, post_ref, send_ref):
    width = gate_ref.shape[1]
    mixed = (gate_ref[...].astype(F32) * value_ref[...].astype(F32)).astype(BF16).T
    grad = (grad_ref[...].astype(F32) * post_ref[...].astype(F32)).astype(BF16).T
    send_ref[:, :CH, :] = mixed.reshape(width // CH, CH, L)
    send_ref[:, CH:, :] = grad.reshape(width // CH, CH, L)


def pre(gate, value, grad, post):
    channels = gate.shape[1]
    width = 1024
    block = pl.BlockSpec((L, width), lambda i: (0, i))
    return pl.pallas_call(
        pre_body,
        grid=(channels // width,),
        in_specs=[block] * 4,
        out_specs=pl.BlockSpec((width // CH, 2 * CH, L), lambda i: (i, 0, 0)),
        out_shape=jax.ShapeDtypeStruct((channels // CH, 2 * CH, L), BF16),
        cost_estimate=pl.CostEstimate(flops=0, bytes_accessed=6 * channels * L * 2, transcendentals=0),
        name="pre",
    )(gate, value, grad, post)


def post_body(back_ref, gate_ref, value_ref, d_pre_ref, d_val_ref):
    width = gate_ref.shape[1]
    back = back_ref[...].reshape(width, L).T.astype(F32)
    d_pre_ref[...] = (back * value_ref[...].astype(F32)).astype(BF16)
    d_val_ref[...] = (back * gate_ref[...].astype(F32)).astype(BF16)


def post(back, gate, value):
    channels = gate.shape[1]
    width = 1024
    block = pl.BlockSpec((L, width), lambda i: (0, i))
    shape = jax.ShapeDtypeStruct((L, channels), BF16)
    return pl.pallas_call(
        post_body,
        grid=(channels // width,),
        in_specs=[pl.BlockSpec((width // CH, CH, L), lambda i: (i, 0, 0)), block, block],
        out_specs=(block, block),
        out_shape=(shape, shape),
        cost_estimate=pl.CostEstimate(flops=0, bytes_accessed=5 * channels * L * 2, transcendentals=0),
        compiler_params=pltpu.CompilerParams(vmem_limit_bytes=VMEM_LIMIT),
        name="post",
    )(back, gate, value)


def channel_of(n, core):
    return lax.div(n, 4) * 8 + core * 4 + lax.rem(n, 4)


def shifts(rows_ref, out):
    lane = lax.broadcasted_iota(jnp.int32, (8, L), 1)
    sub = lax.broadcasted_iota(jnp.int32, (8, L), 0)
    for j in range(R):
        h, i = divmod(j, 8)
        here = rows_ref[pl.ds(8 + j, 8, stride=0), :]
        before = rows_ref[pl.ds(7 + j, 8, stride=0), :]
        shifted = [
            pltpu.roll(jnp.where(lane < L - 8 * p - sub, here, before), 8 * p, 1, stride=1, stride_axis=0)
            for p in range(2)
        ]
        out[h, pl.ds(16 * i, 16), :] = jnp.concatenate(shifted, axis=0).astype(BF16)


def taps_body(core_ref, taps_ref, other_ref, own_ref, *rows):
    core = core_ref[0]
    for r in rows:
        r[pl.ds(0, 8), :] = jnp.zeros((8, L), F32)

    def step(n, _):
        for r, out, side in ((rows[0], other_ref, 1 - core), (rows[1], own_ref, core)):
            r[pl.ds(8, R), :] = taps_ref[channel_of(n, side)].astype(F32)
            shifts(r, out.at[n])
        return 0

    lax.fori_loop(0, CH // 2, step, 0)


def shift_taps(core, taps):
    shape = jax.ShapeDtypeStruct((CH // 2, 8, L, L), BF16)
    return pl.pallas_call(
        taps_body,
        in_specs=[SCALAR, WHOLE],
        out_specs=(WHOLE, WHOLE),
        out_shape=(shape, shape),
        scratch_shapes=[pltpu.VMEM((R + 8, L), F32)] * 2,
        cost_estimate=pl.CostEstimate(flops=0, bytes_accessed=8 << 20, transcendentals=0),
        compiler_params=pltpu.CompilerParams(vmem_limit_bytes=VMEM_LIMIT),
        name="shift_taps",
    )(core, taps)


def correlate(count, load_grad, load_mixed, taps_ref, store, halves):
    lane8 = lax.broadcasted_iota(jnp.int32, (8, L), 1)
    sub8 = lax.broadcasted_iota(jnp.int32, (8, L), 0)
    lane = lax.broadcasted_iota(jnp.int32, (R, L), 1)
    for gp, vp, w, rhs, acc in halves:
        gp[pl.ds(R, 8), :] = jnp.zeros((8, L), F32)
        vp[pl.ds(0, 8), :] = jnp.zeros((8, L), F32)
        w[:, pl.ds(4, 1)] = jnp.zeros((2, 1, L, L), BF16)

    def build(n, half):
        gp, vp, w, rhs, _ = halves[half]
        gp[pl.ds(0, R), :] = load_grad(n)
        vp[pl.ds(8, R), :] = load_mixed(n)
        rows = gp[pl.ds(0, R), :]
        following = gp[pl.ds(1, R), :]
        for u in range(8):
            x = rows
            if u:
                x = pltpu.roll(jnp.where(lane >= 16 * u, rows, following), L - 16 * u, 1)
            even = x.astype(BF16)
            odd = jnp.concatenate([x[8:], jnp.zeros((8, L), F32)], axis=0).astype(BF16)
            for t in range(4):
                w[0, t, pl.ds(16 * u, 16), :] = even[16 * t : 16 * t + 16]
                w[1, t, pl.ds(16 * u, 16), :] = odd[16 * t : 16 * t + 16]
        shifts(vp, rhs)

    def multiply(n, half):
        _, _, w, rhs, acc = halves[half]

        def columns(h):
            pieces = [ref[h, pl.ds(16 * i, 16), :] for i in range(8) for ref in (taps_ref.at[n], rhs)]
            return jnp.concatenate(pieces, axis=0)

        for group in GROUPS:
            depth = 4 - group[0]
            lhs = jnp.concatenate(
                [
                    jnp.concatenate([w[k, min(p + h, 4)] for h in range(depth) for k in range(2)], axis=1)
                    for p in group
                ],
                axis=0,
            )
            cols = jnp.concatenate([columns(h) for h in range(2 * depth)], axis=1)
            out = lax.dot_general(lhs, cols, (((1,), (1,)), ((), ())), preferred_element_type=F32)
            for m, p in enumerate(group):
                acc[0, p] = out[L * m : L * m + L, :L]
                acc[1, p] = out[L * m : L * m + L, L:]

    def finish(n, half):
        _, _, _, _, acc = halves[half]
        tops = []
        for u in range(8):
            lo, hi = ([acc[k, p, pl.ds(16 * u, 16), :] for p in range(4)] for k in range(2))
            lo = [jnp.where(sub8 >= lane8 // 32, lo[0][:8], 0.0), lo[0][8:]] + lo[1:]
            hi = [jnp.where(sub8 >= lane8 // 32 + 4, hi[0][:8], 0.0), hi[0][8:]] + hi[1:]
            tops.append(jnp.concatenate(lo, axis=0) + pltpu.roll(jnp.concatenate(hi, axis=0), R - 4, 0))

        def pair(p, q, width):
            low = (lane & width) == 0
            a = jnp.where(low, p, q)
            b = jnp.where(low, q, p)
            right = pltpu.roll(b, width, 1)
            left = right if 2 * width == L else pltpu.roll(b, L - width, 1)
            return jnp.where(low, a, right) + pltpu.roll(jnp.where(low, left, a), R - width // 32, 0)

        even = pair(pair(tops[0], tops[4], 64), pair(tops[2], tops[6], 64), 32)
        odd = pair(pair(tops[1], tops[5], 64), pair(tops[3], tops[7], 64), 32)
        low = (lane & 16) == 0
        store(n, jnp.where(low, even, pltpu.roll(odd, 16, 1)), jnp.where(low, pltpu.roll(even, L - 16, 1), odd))

    build(0, 0)

    def step(m, _):
        n = 2 * m
        multiply(n, 0)
        build(n + 1, 1)
        finish(jnp.maximum(n - 1, 0), 1)
        multiply(n + 1, 1)
        build(jnp.minimum(n + 2, count - 1), 0)
        finish(n, 0)
        return 0

    lax.fori_loop(0, count // 2, step, 0)
    finish(count - 1, 1)


HALF = [
    pltpu.VMEM((R + 8, L), F32),
    pltpu.VMEM((R + 8, L), F32),
    pltpu.VMEM((2, 5, L, L), BF16),
    pltpu.VMEM((8, L, L), BF16),
    pltpu.VMEM((2, 4, L, L), F32),
]
WHOLE = pl.BlockSpec(memory_space=pltpu.VMEM)
SCALAR = pl.BlockSpec(memory_space=pltpu.SMEM)
CONV_COST = pl.CostEstimate(flops=CH * 256 * 1024 * 256, bytes_accessed=2 << 20, transcendentals=0)
TERMS = jax.ShapeDtypeStruct((CH // 2, R, L), F32)


def other_body(core_ref, recv_ref, taps_ref, term_ref, back_ref, rows_ref, wide, *bufs, scale, batch):
    def widen(r, _):
        at = pl.multiple_of(r * 8, 8)
        for c in range(0, 2 * CH, 16):
            x = recv_ref[pl.ds(at, 8), c : c + 16, :].astype(F32)
            wide[c : c + 16, pl.ds(at, 8), :] = jnp.swapaxes(x, 0, 1)
        return 0

    lax.fori_loop(0, R // 8, widen, 0)

    def keep(c, _):
        rows_ref[c] = wide[c].astype(BF16)
        return 0

    lax.fori_loop(0, 2 * CH, keep, 0, unroll=4)
    side = 1 - core_ref[0]

    def store(n, back, term):
        back_ref[n] = (back * scale).astype(BF16)
        term_ref[n] = term * (scale / batch)

    correlate(
        CH // 2,
        lambda n: wide[CH + channel_of(n, side)],
        lambda n: wide[channel_of(n, side)],
        taps_ref,
        store,
        (bufs[:5], bufs[5:]),
    )


def conv_other(core, recv, taps, scale, batch):
    return pl.pallas_call(
        functools.partial(other_body, scale=scale, batch=batch),
        in_specs=[SCALAR, WHOLE, WHOLE],
        out_specs=(WHOLE,) * 3,
        out_shape=(
            TERMS,
            jax.ShapeDtypeStruct((CH // 2, R, L), BF16),
            jax.ShapeDtypeStruct((2 * CH, R, L), BF16),
        ),
        scratch_shapes=[pltpu.VMEM((2 * CH, R, L), F32)] + HALF * 2,
        cost_estimate=CONV_COST,
        compiler_params=pltpu.CompilerParams(vmem_limit_bytes=VMEM_LIMIT),
        name="conv_other",
    )(core, recv, taps)


def own_body(core_ref, rows_ref, other_ref, taps_ref, term_ref, send_ref, flat, *bufs, scale, batch):
    core = core_ref[0]

    def store(n, back, term):
        flat[channel_of(n, core)] = back * scale
        term_ref[n] = term * (scale / batch)

    correlate(
        CH // 2,
        lambda n: rows_ref[CH + channel_of(n, core)].astype(F32),
        lambda n: rows_ref[channel_of(n, core)].astype(F32),
        taps_ref,
        store,
        (bufs[:5], bufs[5:]),
    )

    def fetch(n, _):
        flat[channel_of(n, 1 - core)] = other_ref[n].astype(F32)
        return 0

    lax.fori_loop(0, CH // 2, fetch, 0, unroll=2)

    def narrow(r, _):
        at = pl.multiple_of(r * 8, 8)
        for c in range(0, CH, 16):
            x = jnp.swapaxes(flat[c : c + 16, pl.ds(at, 8), :], 0, 1)
            send_ref[pl.ds(at, 8), c : c + 16, :] = x.astype(BF16)
        return 0

    lax.fori_loop(0, R // 8, narrow, 0)


def conv_own(core, rows, other, taps, scale, batch):
    return pl.pallas_call(
        functools.partial(own_body, scale=scale, batch=batch),
        in_specs=[SCALAR, WHOLE, WHOLE, WHOLE],
        out_specs=(WHOLE,) * 2,
        out_shape=(TERMS, jax.ShapeDtypeStruct((R, CH, L), BF16)),
        scratch_shapes=[pltpu.VMEM((CH, R, L), F32)] + HALF * 2,
        cost_estimate=CONV_COST,
        compiler_params=pltpu.CompilerParams(vmem_limit_bytes=VMEM_LIMIT),
        name="conv_own",
    )(core, rows, other, taps)


def last_sum_body(own_ref, far_ref, up_ref, down_ref, out_ref):
    total = own_ref[...] + (far_ref[...].astype(F32) + (up_ref[...].astype(F32) + down_ref[...].astype(F32)))
    for r in range(R):
        out_ref[:, pl.ds(L * r, L)] = total[:, r, :]


def last_sum(own, parts):
    return pl.pallas_call(
        last_sum_body,
        in_specs=[WHOLE] * 4,
        out_specs=WHOLE,
        out_shape=jax.ShapeDtypeStruct((own.shape[0], R * L), F32),
        compiler_params=pltpu.CompilerParams(vmem_limit_bytes=VMEM_LIMIT),
        name="last_sum",
    )(own, *parts)


def sum_over_zh(both):
    zh = lax.axis_index("zh")
    count = lax.axis_size("zh")
    pick = functools.partial(lax.dynamic_index_in_dim, axis=0, keepdims=False)
    parts = []
    for shift in (2, 1, 3):
        ahead = [(i, (i + shift) % count) for i in range(count)]
        parts.append(lax.ppermute(pick(both, (zh + shift) % count).astype(BF16), "zh", ahead))
    return last_sum(pick(both, zh), parts)


def local(pre_gate, post_gate, values, conv_out, grad_out, filter_param):
    gate, value, grad = pre_gate[0], values[0], grad_out[0]
    length = filter_param.shape[1]
    exchange = functools.partial(lax.all_to_all, axis_name=CTX, split_axis=0, concat_axis=0, tiled=True)
    scale = length ** (-0.5)
    batch = lax.axis_size("zh") * lax.axis_size("core")
    core = lax.axis_index("core").astype(jnp.int32).reshape(1)
    send = pre(gate, value, grad, post_gate[0])
    recv = exchange(send)
    d_post = (grad.astype(F32) * conv_out[0].astype(F32)).astype(BF16)
    taps_other, taps_own = shift_taps(core, filter_param.reshape(CH, R, L))
    terms, back, rows = conv_other(core, recv, taps_other, scale, batch)
    terms = lax.ppermute(terms, "core", [(0, 1), (1, 0)])
    own, back = conv_own(core, rows, back, taps_own, scale, batch)
    back = exchange(back)
    both = own + terms
    d_filter = sum_over_zh(both.reshape(4, 4, R, L))
    d_pre, d_val = post(back, gate, value)
    return (d_pre[None], d_post[None], d_val[None], d_filter)


def solution(mesh):
    fine = Mesh(mesh.devices.reshape(4, 2, 4, 4, 4), DP + CTX)
    tokens = P(DP, CTX, None)
    return jax.shard_map(
        local,
        mesh=fine,
        in_specs=(tokens,) * 5 + (P(CTX, None),),
        out_specs=(tokens, tokens, tokens, P(CTX + DP, None)),
        check_vma=False,
    )
```

```python
import functools

import jax
import jax.numpy as jnp
from jax import lax
from jax.experimental import pallas as pl
from jax.experimental.pallas import tpu as pltpu
from jax.sharding import Mesh
from jax.sharding import PartitionSpec as P


L = 128
R = 64
CH = 32
DP = ("zh", "core")
CTX = ("zl", "y", "x")
F32 = jnp.float32
BF16 = jnp.bfloat16
VMEM_LIMIT = 16 << 20
GROUPS = ((0, 1), (2, 3))


def pre_body(gate_ref, value_ref, grad_ref, post_ref, send_ref):
    width = gate_ref.shape[1]
    mixed = (gate_ref[...].astype(F32) * value_ref[...].astype(F32)).astype(BF16).T
    grad = (grad_ref[...].astype(F32) * post_ref[...].astype(F32)).astype(BF16).T
    send_ref[:, :CH, :] = mixed.reshape(width // CH, CH, L)
    send_ref[:, CH:, :] = grad.reshape(width // CH, CH, L)


def pre(gate, value, grad, post):
    channels = gate.shape[1]
    width = 1024
    block = pl.BlockSpec((L, width), lambda i: (0, i))
    return pl.pallas_call(
        pre_body,
        grid=(channels // width,),
        in_specs=[block] * 4,
        out_specs=pl.BlockSpec((width // CH, 2 * CH, L), lambda i: (i, 0, 0)),
        out_shape=jax.ShapeDtypeStruct((channels // CH, 2 * CH, L), BF16),
        cost_estimate=pl.CostEstimate(flops=0, bytes_accessed=6 * channels * L * 2, transcendentals=0),
        name="pre",
    )(gate, value, grad, post)


def post_body(back_ref, gate_ref, value_ref, d_pre_ref, d_val_ref):
    width = gate_ref.shape[1]
    back = back_ref[...].reshape(width, L).T.astype(F32)
    d_pre_ref[...] = (back * value_ref[...].astype(F32)).astype(BF16)
    d_val_ref[...] = (back * gate_ref[...].astype(F32)).astype(BF16)


def post(back, gate, value):
    channels = gate.shape[1]
    width = 1024
    block = pl.BlockSpec((L, width), lambda i: (0, i))
    shape = jax.ShapeDtypeStruct((L, channels), BF16)
    return pl.pallas_call(
        post_body,
        grid=(channels // width,),
        in_specs=[pl.BlockSpec((width // CH, CH, L), lambda i: (i, 0, 0)), block, block],
        out_specs=(block, block),
        out_shape=(shape, shape),
        cost_estimate=pl.CostEstimate(flops=0, bytes_accessed=5 * channels * L * 2, transcendentals=0),
        compiler_params=pltpu.CompilerParams(vmem_limit_bytes=VMEM_LIMIT),
        name="post",
    )(back, gate, value)


def channel_of(n, core):
    return lax.div(n, 4) * 8 + core * 4 + lax.rem(n, 4)


def shifts(rows_ref, out):
    lane = lax.broadcasted_iota(jnp.int32, (8, L), 1)
    sub = lax.broadcasted_iota(jnp.int32, (8, L), 0)
    for j in range(R):
        h, i = divmod(j, 8)
        here = rows_ref[pl.ds(8 + j, 8, stride=0), :]
        before = rows_ref[pl.ds(7 + j, 8, stride=0), :]
        shifted = [
            pltpu.roll(jnp.where(lane < L - 8 * p - sub, here, before), 8 * p, 1, stride=1, stride_axis=0)
            for p in range(2)
        ]
        out[h, pl.ds(16 * i, 16), :] = jnp.concatenate(shifted, axis=0).astype(BF16)


def taps_body(core_ref, taps_ref, other_ref, own_ref, *rows):
    core = core_ref[0]
    for r in rows:
        r[pl.ds(0, 8), :] = jnp.zeros((8, L), F32)

    def step(n, _):
        for r, out, side in ((rows[0], other_ref, 1 - core), (rows[1], own_ref, core)):
            r[pl.ds(8, R), :] = taps_ref[channel_of(n, side)].astype(F32)
            shifts(r, out.at[n])
        return 0

    lax.fori_loop(0, CH // 2, step, 0)


def shift_taps(core, taps):
    shape = jax.ShapeDtypeStruct((CH // 2, 8, L, L), BF16)
    return pl.pallas_call(
        taps_body,
        in_specs=[SCALAR, WHOLE],
        out_specs=(WHOLE, WHOLE),
        out_shape=(shape, shape),
        scratch_shapes=[pltpu.VMEM((R + 8, L), F32)] * 2,
        cost_estimate=pl.CostEstimate(flops=0, bytes_accessed=8 << 20, transcendentals=0),
        compiler_params=pltpu.CompilerParams(vmem_limit_bytes=VMEM_LIMIT),
        name="shift_taps",
    )(core, taps)


def correlate(count, load_grad, load_mixed, taps_ref, store, halves):
    lane8 = lax.broadcasted_iota(jnp.int32, (8, L), 1)
    sub8 = lax.broadcasted_iota(jnp.int32, (8, L), 0)
    lane = lax.broadcasted_iota(jnp.int32, (R, L), 1)
    for gp, vp, w, rhs, acc in halves:
        gp[pl.ds(R, 8), :] = jnp.zeros((8, L), F32)
        vp[pl.ds(0, 8), :] = jnp.zeros((8, L), F32)
        w[:, pl.ds(4, 1)] = jnp.zeros((2, 1, L, L), BF16)

    def build(n, half):
        gp, vp, w, rhs, _ = halves[half]
        gp[pl.ds(0, R), :] = load_grad(n)
        vp[pl.ds(8, R), :] = load_mixed(n)
        rows = gp[pl.ds(0, R), :]
        following = gp[pl.ds(1, R), :]
        for u in range(8):
            x = rows
            if u:
                x = pltpu.roll(jnp.where(lane >= 16 * u, rows, following), L - 16 * u, 1)
            even = x.astype(BF16)
            odd = jnp.concatenate([x[8:], jnp.zeros((8, L), F32)], axis=0).astype(BF16)
            for t in range(4):
                w[0, t, pl.ds(16 * u, 16), :] = even[16 * t : 16 * t + 16]
                w[1, t, pl.ds(16 * u, 16), :] = odd[16 * t : 16 * t + 16]
        shifts(vp, rhs)

    def multiply(n, half):
        _, _, w, rhs, acc = halves[half]

        def columns(h):
            pieces = [ref[h, pl.ds(16 * i, 16), :] for i in range(8) for ref in (taps_ref.at[n], rhs)]
            return jnp.concatenate(pieces, axis=0)

        for group in GROUPS:
            depth = 4 - group[0]
            lhs = jnp.concatenate(
                [
                    jnp.concatenate([w[k, min(p + h, 4)] for h in range(depth) for k in range(2)], axis=1)
                    for p in group
                ],
                axis=0,
            )
            cols = jnp.concatenate([columns(h) for h in range(2 * depth)], axis=1)
            out = lax.dot_general(lhs, cols, (((1,), (1,)), ((), ())), preferred_element_type=F32)
            for m, p in enumerate(group):
                acc[0, p] = out[L * m : L * m + L, :L]
                acc[1, p] = out[L * m : L * m + L, L:]

    def finish(n, half):
        _, _, _, _, acc = halves[half]
        tops = []
        for u in range(8):
            lo, hi = ([acc[k, p, pl.ds(16 * u, 16), :] for p in range(4)] for k in range(2))
            lo = [jnp.where(sub8 >= lane8 // 32, lo[0][:8], 0.0), lo[0][8:]] + lo[1:]
            hi = [jnp.where(sub8 >= lane8 // 32 + 4, hi[0][:8], 0.0), hi[0][8:]] + hi[1:]
            tops.append(jnp.concatenate(lo, axis=0) + pltpu.roll(jnp.concatenate(hi, axis=0), R - 4, 0))

        def pair(p, q, width):
            low = (lane & width) == 0
            a = jnp.where(low, p, q)
            b = jnp.where(low, q, p)
            right = pltpu.roll(b, width, 1)
            left = right if 2 * width == L else pltpu.roll(b, L - width, 1)
            return jnp.where(low, a, right) + pltpu.roll(jnp.where(low, left, a), R - width // 32, 0)

        even = pair(pair(tops[0], tops[4], 64), pair(tops[2], tops[6], 64), 32)
        odd = pair(pair(tops[1], tops[5], 64), pair(tops[3], tops[7], 64), 32)
        low = (lane & 16) == 0
        store(n, jnp.where(low, even, pltpu.roll(odd, 16, 1)), jnp.where(low, pltpu.roll(even, L - 16, 1), odd))

    build(0, 0)

    def step(m, _):
        n = 2 * m
        multiply(n, 0)
        build(n + 1, 1)
        finish(jnp.maximum(n - 1, 0), 1)
        multiply(n + 1, 1)
        build(jnp.minimum(n + 2, count - 1), 0)
        finish(n, 0)
        return 0

    lax.fori_loop(0, count // 2, step, 0)
    finish(count - 1, 1)


HALF = [
    pltpu.VMEM((R + 8, L), F32),
    pltpu.VMEM((R + 8, L), F32),
    pltpu.VMEM((2, 5, L, L), BF16),
    pltpu.VMEM((8, L, L), BF16),
    pltpu.VMEM((2, 4, L, L), F32),
]
WHOLE = pl.BlockSpec(memory_space=pltpu.VMEM)
SCALAR = pl.BlockSpec(memory_space=pltpu.SMEM)
CONV_COST = pl.CostEstimate(flops=CH * 256 * 1024 * 256, bytes_accessed=2 << 20, transcendentals=0)
TERMS = jax.ShapeDtypeStruct((CH // 2, R, L), F32)


def other_body(core_ref, recv_ref, taps_ref, term_ref, back_ref, rows_ref, wide, *bufs, scale, batch):
    def widen(r, _):
        at = pl.multiple_of(r * 8, 8)
        for c in range(0, 2 * CH, 16):
            x = recv_ref[pl.ds(at, 8), c : c + 16, :].astype(F32)
            x = jnp.swapaxes(x, 0, 1)
            wide[c : c + 16, pl.ds(at, 8), :] = x
            rows_ref[c : c + 16, pl.ds(at, 8), :] = x.astype(BF16)
        return 0

    lax.fori_loop(0, R // 8, widen, 0, unroll=2)
    side = 1 - core_ref[0]

    def store(n, back, term):
        back_ref[n] = (back * scale).astype(BF16)
        term_ref[n] = term * (scale / batch)

    correlate(
        CH // 2,
        lambda n: wide[CH + channel_of(n, side)],
        lambda n: wide[channel_of(n, side)],
        taps_ref,
        store,
        (bufs[:5], bufs[5:]),
    )


def conv_other(core, recv, taps, scale, batch):
    return pl.pallas_call(
        functools.partial(other_body, scale=scale, batch=batch),
        in_specs=[SCALAR, WHOLE, WHOLE],
        out_specs=(WHOLE,) * 3,
        out_shape=(
            TERMS,
            jax.ShapeDtypeStruct((CH // 2, R, L), BF16),
            jax.ShapeDtypeStruct((2 * CH, R, L), BF16),
        ),
        scratch_shapes=[pltpu.VMEM((2 * CH, R, L), F32)] + HALF * 2,
        cost_estimate=CONV_COST,
        compiler_params=pltpu.CompilerParams(vmem_limit_bytes=VMEM_LIMIT),
        name="conv_other",
    )(core, recv, taps)


def own_body(core_ref, rows_ref, other_ref, taps_ref, term_ref, send_ref, flat, *bufs, scale, batch):
    core = core_ref[0]

    def store(n, back, term):
        flat[channel_of(n, core)] = back * scale
        term_ref[n] = term * (scale / batch)

    correlate(
        CH // 2,
        lambda n: rows_ref[CH + channel_of(n, core)].astype(F32),
        lambda n: rows_ref[channel_of(n, core)].astype(F32),
        taps_ref,
        store,
        (bufs[:5], bufs[5:]),
    )

    def fetch(n, _):
        flat[channel_of(n, 1 - core)] = other_ref[n].astype(F32)
        return 0

    lax.fori_loop(0, CH // 2, fetch, 0, unroll=2)

    def narrow(r, _):
        at = pl.multiple_of(r * 8, 8)
        for c in range(0, CH, 16):
            x = jnp.swapaxes(flat[c : c + 16, pl.ds(at, 8), :], 0, 1)
            send_ref[pl.ds(at, 8), c : c + 16, :] = x.astype(BF16)
        return 0

    lax.fori_loop(0, R // 8, narrow, 0, unroll=2)


def conv_own(core, rows, other, taps, scale, batch):
    return pl.pallas_call(
        functools.partial(own_body, scale=scale, batch=batch),
        in_specs=[SCALAR, WHOLE, WHOLE, WHOLE],
        out_specs=(WHOLE,) * 2,
        out_shape=(TERMS, jax.ShapeDtypeStruct((R, CH, L), BF16)),
        scratch_shapes=[pltpu.VMEM((CH, R, L), F32)] + HALF * 2,
        cost_estimate=CONV_COST,
        compiler_params=pltpu.CompilerParams(vmem_limit_bytes=VMEM_LIMIT),
        name="conv_own",
    )(core, rows, other, taps)


def last_sum_body(own_ref, far_ref, up_ref, down_ref, out_ref):
    total = own_ref[...] + (far_ref[...].astype(F32) + (up_ref[...].astype(F32) + down_ref[...].astype(F32)))
    for r in range(R):
        out_ref[:, pl.ds(L * r, L)] = total[:, r, :]


def last_sum(own, parts):
    return pl.pallas_call(
        last_sum_body,
        in_specs=[WHOLE] * 4,
        out_specs=WHOLE,
        out_shape=jax.ShapeDtypeStruct((own.shape[0], R * L), F32),
        compiler_params=pltpu.CompilerParams(vmem_limit_bytes=VMEM_LIMIT),
        name="last_sum",
    )(own, *parts)


def sum_over_zh(both):
    zh = lax.axis_index("zh")
    count = lax.axis_size("zh")
    pick = functools.partial(lax.dynamic_index_in_dim, axis=0, keepdims=False)
    parts = []
    for shift in (2, 1, 3):
        ahead = [(i, (i + shift) % count) for i in range(count)]
        parts.append(lax.ppermute(pick(both, (zh + shift) % count).astype(BF16), "zh", ahead))
    return last_sum(pick(both, zh), parts)


def local(pre_gate, post_gate, values, conv_out, grad_out, filter_param):
    gate, value, grad = pre_gate[0], values[0], grad_out[0]
    length = filter_param.shape[1]
    exchange = functools.partial(lax.all_to_all, axis_name=CTX, split_axis=0, concat_axis=0, tiled=True)
    scale = length ** (-0.5)
    batch = lax.axis_size("zh") * lax.axis_size("core")
    core = lax.axis_index("core").astype(jnp.int32).reshape(1)
    send = pre(gate, value, grad, post_gate[0])
    recv = exchange(send)
    d_post = (grad.astype(F32) * conv_out[0].astype(F32)).astype(BF16)
    taps_other, taps_own = shift_taps(core, filter_param.reshape(CH, R, L))
    terms, back, rows = conv_other(core, recv, taps_other, scale, batch)
    terms = lax.ppermute(terms, "core", [(0, 1), (1, 0)])
    own, back = conv_own(core, rows, back, taps_own, scale, batch)
    back = exchange(back)
    both = own + terms
    d_filter = sum_over_zh(both.reshape(4, 4, R, L))
    d_pre, d_val = post(back, gate, value)
    return (d_pre[None], d_post[None], d_val[None], d_filter)


def solution(mesh):
    fine = Mesh(mesh.devices.reshape(4, 2, 4, 4, 4), DP + CTX)
    tokens = P(DP, CTX, None)
    return jax.shard_map(
        local,
        mesh=fine,
        in_specs=(tokens,) * 5 + (P(CTX, None),),
        out_specs=(tokens, tokens, tokens, P(CTX + DP, None)),
        check_vma=False,
    )
```
